256 devices in a mesh: blk: 32 (over x_lo, z, core), head: 8 (over y, x_hi).
Axes of the slice: x: 4 (x_hi: 2, x_lo: 2; x = x_hi * 2 + x_lo), y: 4, z: 8, core: 2. Of those that a mesh axis runs over, the one named last changes fastest.
Arguments:
- queries: bfloat16 [2, 4096, 32, 128], P(None, 'blk', 'head'), may hold values from -30 to 30
- new_keys: bfloat16 [2, 4096, 16, 128], P(None, 'blk', 'head'), may hold values from -30 to 30
- new_values: bfloat16 [2, 4096, 16, 128], P(None, 'blk', 'head'), may hold values from -6 to 6
- pool_keys: bfloat16 [64, 128, 16, 128], P('blk', None, 'head'), may hold values from -30 to 30
- pool_values: bfloat16 [64, 128, 16, 128], P('blk', None, 'head'), may hold values from -6 to 6
- page_table: int32 [2, 32], replicated, may hold values from 0 to 63, as said below
- cache_len: int32 [2], replicated, may hold values from 1024 to 4096, as said below
- out_weight: bfloat16 [32, 128, 4608], P('head'), may hold values from -0.09375 to 0.09375
- residual: bfloat16 [2, 4096, 4608], P(None, ('blk', 'head')), may hold values from -6 to 6
- post_gain: float32 [4608], replicated, may hold values from 0.1 to 1.9
Outputs:
- mixed: bfloat16 [2, 4096, 4608], P(None, ('blk', 'head'))
The draws below stay inside these ranges and needn't reach their ends.
Inputs may be any that keep to these rules, and one draw needn't show every extreme that they name: `page_table`: every pool page appears exactly once in the table. `cache_len`: one request has exactly 4096 cached tokens.
All inputs are finite; a program needn't handle non-finite values.
Results may differ from the reference program's by a relative error of at most 0.015.
Values may be sent and summed in bfloat16 or wider, within the bound.
A program may use at most 128 MiB of HBM per device.

```python
import jax
import jax.numpy as jnp
from jax import lax

D = 4608
QH = 32
KVH = 16
HD = 128
PAGE = 128
REQ = 2
TOK_DEV = 256
NEW = 4096
POOL = 64
MAXP = 32


def draw_page_table(key, part):
    order = jax.random.permutation(key, REQ * MAXP)
    return order.reshape(REQ, MAXP).astype(jnp.int32)


def draw_cache_len(key, part):
    full_len = MAXP * PAGE
    chosen = jax.random.randint(jax.random.fold_in(key, 11), (), 0, REQ)
    others = jax.random.randint(jax.random.fold_in(key, 12), (REQ,), full_len // 4, full_len + 1)
    return jnp.where(jnp.arange(REQ) == chosen, full_len, others).astype(jnp.int32)


def block_scale(key, shape, cuts, smallest, top_value):
    def one(dim, parts):
        heights = jax.random.uniform(jax.random.fold_in(jax.random.fold_in(key, 6), dim), (parts,), jnp.float32, smallest / len(cuts), top_value / len(cuts))
        return jnp.repeat(jnp.exp(heights), shape[dim] // parts).reshape((-1,) + (1,) * (len(shape) - dim - 1))

    gain = one(*cuts[0])
    for cut in cuts[1:]:
        gain = gain * one(*cut)
    return gain


def normal_values(own_key, extent, width, most, shards=(), held_as=jnp.bfloat16):
    level = block_scale(own_key, extent, shards, -0.22, 0.18) if shards else 1.0
    values = jax.random.normal(own_key, extent, jnp.float32) * width * level
    return jnp.minimum(jnp.maximum(values, -most), most).astype(held_as)


def setup_inputs(seed: int = 0) -> dict:
    arg_keys = jax.random.split(jax.random.key(seed), 11)
    queries = normal_values(arg_keys[0], (REQ, NEW, QH, HD), 5.0, 30.0, ((1, 32), (2, 8)))
    new_keys = normal_values(arg_keys[1], (REQ, NEW, KVH, HD), 5.0, 30.0, ((1, 32), (2, 8)))
    new_values = normal_values(arg_keys[2], (REQ, NEW, KVH, HD), 1.0, 6.0, ((1, 32), (2, 8)))
    pool_keys = normal_values(arg_keys[3], (POOL, PAGE, KVH, HD), 5.0, 30.0, ((0, 32), (2, 8)))
    pool_values = normal_values(arg_keys[4], (POOL, PAGE, KVH, HD), 1.0, 6.0, ((0, 32), (2, 8)))
    page_table = draw_page_table(jax.random.fold_in(arg_keys[10], 71), 0)
    cache_len = draw_cache_len(jax.random.fold_in(arg_keys[10], 71), 0)
    out_weight = normal_values(arg_keys[7], (QH, HD, D), (QH * HD) ** -0.5, 0.09375, ((0, 8),))
    residual = normal_values(arg_keys[8], (REQ, NEW, D), 1.0, 6.0, ((1, 256),))
    post_gain = jnp.clip(1.0 + 0.18 * jax.random.normal(arg_keys[9], (D,), jnp.float32), 0.1, 1.9)
    return dict(queries=queries, new_keys=new_keys, new_values=new_values, pool_keys=pool_keys, pool_values=pool_values, page_table=page_table, cache_len=cache_len, out_weight=out_weight, residual=residual, post_gain=post_gain)


soft_cap = 50.0
score_scale = 144.0 ** (-0.5)
norm_eps = 1e-06

def reference(queries, new_keys, new_values, pool_keys, pool_values, page_table, cache_len, out_weight, residual, post_gain):
    group = QH // KVH
    cache_tokens = MAXP * PAGE
    attended_all = []
    for request in range(REQ):
        slots = page_table[request].astype(jnp.int32)
        cache_k = pool_keys[slots].reshape(cache_tokens, KVH, HD)
        cache_v = pool_values[slots].reshape(cache_tokens, KVH, HD)
        key_all = jnp.concatenate([cache_k, new_keys[request]], 0).astype(jnp.float32)
        value_all = jnp.concatenate([cache_v, new_values[request]], 0).astype(jnp.float32)
        cache_ok = jnp.arange(cache_tokens, dtype=jnp.int32) < cache_len[request]
        query_req = queries[request].reshape(NEW // TOK_DEV, TOK_DEV, KVH, group, HD)

        def block_attend(inputs):
            query_block, block_index = inputs
            query_index = block_index * TOK_DEV + jnp.arange(TOK_DEV, dtype=jnp.int32)
            new_ok = jnp.arange(NEW, dtype=jnp.int32)[None, :] <= query_index[:, None]
            valid_keys = jnp.concatenate([jnp.broadcast_to(cache_ok[None, :], (TOK_DEV, cache_tokens)), new_ok], 1)
            scores = jnp.einsum('tkgd,skd->kgts', query_block.astype(jnp.float32), key_all, precision=lax.Precision.HIGHEST) * score_scale
            capped = soft_cap * jnp.tanh(scores / soft_cap)
            weights = jnp.where(valid_keys[None, None], jnp.exp(capped), 0.0).astype(jnp.bfloat16)
            weights = lax.optimization_barrier(weights).astype(jnp.float32)
            numerator = jnp.einsum('kgts,skd->tkgd', weights, value_all, precision=lax.Precision.HIGHEST)
            denominator = lax.optimization_barrier(jnp.sum(weights, axis=-1))
            return (numerator / jnp.transpose(denominator, (2, 0, 1))[..., None]).astype(jnp.bfloat16)
        blocks_out = lax.map(block_attend, (query_req, jnp.arange(NEW // TOK_DEV, dtype=jnp.int32)))
        attended_all.append(blocks_out.reshape(NEW, QH * HD))
    attended = jnp.concatenate(attended_all, 0)
    projected = jnp.dot(attended, out_weight.reshape(QH * HD, D), preferred_element_type=jnp.float32)
    inv_rms = lax.rsqrt(lax.optimization_barrier(jnp.mean(projected * projected, axis=-1, keepdims=True)) + norm_eps)
    mixed_out = residual.reshape(REQ * NEW, D).astype(jnp.float32) + post_gain * projected * inv_rms
    return mixed_out.reshape(REQ, NEW, D).astype(jnp.bfloat16)
```

```python
import functools

import jax
import jax.numpy as jnp
from jax import lax
from jax.experimental import pallas as pl
from jax.experimental.pallas import tpu as pltpu
from jax.sharding import PartitionSpec as P

soft_cap = 50.0
score_scale = 144.0 ** (-0.5)
norm_eps = 1e-06

MESH_ID = pl.DeviceIdType.MESH


def attend_kernel(
    zs_n,
    tok,
    kv_hbm,
    q_hbm,
    mask_ref,
    out_ref,
    kvbuf,
    qall,
    acc,
    att_send,
    att_recv,
    local_sem,
    send_sem,
    recv_sem,
    x_send,
    x_recv,
):
    blk = lax.axis_index("blk")
    me_c = lax.rem(blk, 2)
    me_z = lax.rem(blk // 2, zs_n)
    me_x = blk // (2 * zs_n)

    def place(x, z, c):
        return {"blk": (x * zs_n + z) * 2 + c}

    right = place(me_x, lax.rem(me_z + 1, zs_n), me_c)
    left = place(me_x, lax.rem(me_z + zs_n - 1, zs_n), me_c)
    sibling = place(me_x, me_z, 1 - me_c)
    partner = place(1 - me_x, me_z, me_c)

    barrier = pltpu.get_barrier_semaphore()
    for other in (right, left, sibling, partner):
        pl.semaphore_signal(barrier, inc=1, device_id=other, device_id_type=MESH_ID)

    own_kv = pltpu.make_async_copy(kv_hbm.at[me_x], kvbuf.at[me_c, me_x, me_z], local_sem.at[0])
    own_q = pltpu.make_async_copy(q_hbm.at[me_x], qall.at[me_x], local_sem.at[1])
    own_kv.start()
    own_q.start()
    pl.semaphore_wait(barrier, 4)

    q_swap = pltpu.make_async_remote_copy(
        src_ref=q_hbm.at[1 - me_x],
        dst_ref=qall.at[me_x],
        send_sem=x_send.at[0],
        recv_sem=x_recv.at[0],
        device_id=partner,
        device_id_type=MESH_ID,
    )
    kv_swap = pltpu.make_async_remote_copy(
        src_ref=kv_hbm.at[1 - me_x],
        dst_ref=kvbuf.at[me_c, me_x, me_z],
        send_sem=x_send.at[1],
        recv_sem=recv_sem.at[me_c, me_x, me_z],
        device_id=partner,
        device_id_type=MESH_ID,
    )
    q_swap.start()
    kv_swap.start()

    def forward(way, device, x, z):
        return pltpu.make_async_remote_copy(
            src_ref=kvbuf.at[me_c, x, z],
            dst_ref=kvbuf.at[me_c, x, z],
            send_sem=send_sem.at[way, x, z],
            recv_sem=recv_sem.at[me_c, x, z],
            device_id=device,
            device_id_type=MESH_ID,
        )

    def landed(c, x, z):
        pltpu.make_async_remote_copy(
            src_ref=kvbuf.at[c, x, z],
            dst_ref=kvbuf.at[c, x, z],
            send_sem=x_send.at[1],
            recv_sem=recv_sem.at[c, x, z],
            device_id=sibling,
            device_id_type=MESH_ID,
        ).wait_recv()

    half = zs_n // 2
    last = zs_n

    def steps_right(k):
        is_b = (lax.rem(k, 2) == 0) & (k > 0)
        dist = jnp.where(lax.rem(k, 2) == 1, (k + 1) // 2, jnp.maximum(k - 2, 0) // 2)
        x = jnp.where(is_b, 1 - me_x, me_x)
        return x, lax.rem(me_z - dist + zs_n, zs_n)

    def steps_left(k):
        is_b = ((lax.rem(k, 2) == 0) & (k > 0)) | (k == last - 1)
        dist = jnp.where(lax.rem(k, 2) == 1, (k + 1) // 2, jnp.maximum(k - 2, 0) // 2)
        dist = jnp.where(k >= last - 1, k - (last - half), dist)
        x = jnp.where(is_b, 1 - me_x, me_x)
        return x, lax.rem(me_z + dist, zs_n)

    def goes_right(k):
        return k <= last - 2

    def goes_left(k):
        return (k != last - 3) & (k != last)

    def is_own(k):
        return (k == 0) | (k == 2)

    rows = 2 * tok
    lane = lax.broadcasted_iota(jnp.int32, (rows, tok), 1)
    row = lax.broadcasted_iota(jnp.int32, (rows, tok), 0)
    ahead = lax.rem(row, tok) - lane

    def weigh(scores):
        capped = jnp.tanh(scores * (score_scale / soft_cap)) * soft_cap
        return jnp.exp(capped)

    ones = jnp.ones((3 * tok, 128), jnp.bfloat16)

    def dots(a, b):
        return lax.dot_general(
            a, b, (((1,), (1,)), ((), ())), preferred_element_type=jnp.float32
        )

    def attend(c, x, z):
        key_block = (x * zs_n + z) * 2 + c
        seen = mask_ref[key_block]
        for r in range(2):
            pool = pl.ds(tok, 2 * tok)
            new = pl.ds(r * 3 * tok, tok)
            every = pl.ds(r * tok, 3 * tok)
            pool_k = kvbuf[c, x, z, 0, pool, :]
            new_k = kvbuf[c, x, z, 0, new, :]
            values = jnp.concatenate([kvbuf[c, x, z, 1, every, :], ones], axis=1)
            for qx in range(2):
                query = qall[qx, r]
                query_block = (qx * zs_n + me_z) * 2 + me_c
                w_pool = weigh(dots(query, pool_k)) * seen[r : r + 1, :]
                w_new = jnp.where(
                    ahead >= (key_block - query_block) * tok, weigh(dots(query, new_k)), 0.0
                )
                both = [w_new, w_pool] if r == 0 else [w_pool, w_new]
                weights = jnp.concatenate(both, axis=1).astype(jnp.bfloat16)
                acc[qx, r] += jnp.dot(weights, values, preferred_element_type=jnp.float32)

    own_kv.wait()
    acc[...] = jnp.zeros_like(acc)

    def one_step(k, carry):
        rx, rz = steps_right(k)
        lx, lz = steps_left(k)
        own = is_own(k)

        @pl.when(k > 0)
        def _():
            landed(me_c, rx, rz)

        @pl.when(goes_right(k))
        def _():
            forward(0, right, rx, rz).start()

        @pl.when(jnp.logical_not(own))
        def _():
            landed(me_c, lx, lz)

        @pl.when(goes_left(k))
        def _():
            forward(1, left, lx, lz).start()

        forward(2, sibling, rx, rz).start()

        @pl.when(jnp.logical_not(own))
        def _():
            forward(2, sibling, lx, lz).start()

        @pl.when(k == 0)
        def _():
            own_q.wait()
            q_swap.wait_recv()

        def one_shard(i, carry):
            c = jnp.where(i % 2 == 0, me_c, 1 - me_c)
            x = jnp.where(i < 2, rx, lx)
            z = jnp.where(i < 2, rz, lz)

            @pl.when(i % 2 == 1)
            def _():
                landed(c, x, z)

            attend(c, x, z)
            return carry

        lax.fori_loop(0, jnp.where(own, 2, 4), one_shard, 0)
        return carry

    lax.fori_loop(0, last + 1, one_step, 0)

    def finished(qx, r):
        total = acc[qx, r]
        return (total[:, :128] / total[:, 128:]).astype(jnp.bfloat16)

    for r in range(2):
        att_send[r] = finished(1 - me_x, r)
    att_swap = pltpu.make_async_remote_copy(
        src_ref=att_send,
        dst_ref=att_recv,
        send_sem=x_send.at[2],
        recv_sem=x_recv.at[1],
        device_id=partner,
        device_id_type=MESH_ID,
    )
    att_swap.start()

    share = tok // 8

    def put(x, r, value):
        for g in range(2):
            columns = pl.ds(pl.multiple_of((2 * x + g) * 128, 128), 128)
            out_ref[:, r, :, columns] = value[g * tok : (g + 1) * tok].reshape(8, share, 128)

    for r in range(2):
        put(me_x, r, finished(me_x, r))
    att_swap.wait()
    for r in range(2):
        put(1 - me_x, r, att_recv[r])

    q_swap.wait_send()
    kv_swap.wait_send()

    def drain(k, carry):
        rx, rz = steps_right(k)
        lx, lz = steps_left(k)

        @pl.when(goes_right(k))
        def _():
            forward(0, right, rx, rz).wait_send()

        @pl.when(goes_left(k))
        def _():
            forward(1, left, lx, lz).wait_send()

        forward(2, sibling, rx, rz).wait_send()

        @pl.when(jnp.logical_not(is_own(k)))
        def _():
            forward(2, sibling, lx, lz).wait_send()

        return carry

    lax.fori_loop(0, last + 1, drain, 0)


def gather_and_attend(queries, new_keys, new_values, pool_keys, pool_values, page_table, cache_len):
    req, tok, heads, dim = queries.shape
    kv_heads = new_keys.shape[2]
    zs_n = lax.axis_size("blk") // 4

    def laid(new, pool):
        new = new.transpose(2, 0, 1, 3)
        pool = pool.transpose(2, 0, 1, 3).reshape(kv_heads, 2 * tok, dim)
        return jnp.concatenate([new[:, 0], pool, new[:, 1]], axis=1)

    kv = jnp.stack([laid(new_keys, pool_keys), laid(new_values, pool_values)], axis=1)
    q = queries.reshape(req, tok, kv_heads, heads // kv_heads, dim)
    q = q.transpose(2, 0, 3, 1, 4).reshape(kv_heads, req, 2 * tok, dim)

    pages = 2 * lax.axis_size("blk")
    slots = page_table.shape[1]
    match = jnp.arange(pages, dtype=jnp.int32)[:, None, None] == page_table[None]
    slot = jnp.sum(jnp.where(match, jnp.arange(slots, dtype=jnp.int32), 0), axis=2)
    owned = jnp.any(match, axis=2)
    position = slot[:, :, None] * tok + jnp.arange(tok, dtype=jnp.int32)
    seen = (owned[:, :, None] & (position < cache_len[None, :, None])).astype(jnp.float32)
    seen = seen.reshape(pages // 2, 2, req, tok).transpose(0, 2, 1, 3)
    seen = seen.reshape(pages // 2, req, 2 * tok)

    hbm = pl.BlockSpec(memory_space=pl.ANY)
    vmem = pl.BlockSpec(memory_space=pltpu.VMEM)
    return pl.pallas_call(
        functools.partial(attend_kernel, zs_n, tok),
        name="gather_and_attend",
        out_shape=jax.ShapeDtypeStruct((8, req, tok // 8, heads * dim), jnp.bfloat16),
        in_specs=[hbm, hbm, vmem],
        out_specs=vmem,
        scratch_shapes=[
            pltpu.VMEM((2, 2, zs_n, 2, 4 * tok, dim), jnp.bfloat16),
            pltpu.VMEM((2, req, 2 * tok, dim), jnp.bfloat16),
            pltpu.VMEM((2, req, 2 * tok, 2 * dim), jnp.float32),
            pltpu.VMEM((req, 2 * tok, dim), jnp.bfloat16),
            pltpu.VMEM((req, 2 * tok, dim), jnp.bfloat16),
            pltpu.SemaphoreType.DMA((2,)),
            pltpu.SemaphoreType.DMA((3, 2, zs_n)),
            pltpu.SemaphoreType.DMA((2, 2, zs_n)),
            pltpu.SemaphoreType.DMA((3,)),
            pltpu.SemaphoreType.DMA((2,)),
        ],
        compiler_params=pltpu.CompilerParams(collective_id=0, has_side_effects=True),
    )(kv, q, seen)


def shards(
    queries,
    new_keys,
    new_values,
    pool_keys,
    pool_values,
    page_table,
    cache_len,
    out_weight,
    residual,
    post_gain,
):
    req, tok, heads, dim = queries.shape
    attended = gather_and_attend(
        queries, new_keys, new_values, pool_keys, pool_values, page_table, cache_len
    )
    share = tok // lax.axis_size("head")
    attended = attended.reshape(req * tok, heads * dim)
    weight_rows = out_weight.reshape(heads * dim, out_weight.shape[2])
    projected = lax.psum_scatter(
        jnp.dot(attended, weight_rows, preferred_element_type=jnp.float32).astype(jnp.bfloat16),
        "head",
        scatter_dimension=0,
        tiled=True,
    ).astype(jnp.float32)
    projected = projected.reshape(req, share, projected.shape[1])
    inv_rms = lax.rsqrt(jnp.mean(projected * projected, axis=-1, keepdims=True) + norm_eps)
    mixed_out = residual.astype(jnp.float32) + post_gain * projected * inv_rms
    return mixed_out.astype(jnp.bfloat16)


def solution(mesh):
    placed = (
        P(None, "blk", "head", None),
        P(None, "blk", "head", None),
        P(None, "blk", "head", None),
        P("blk", None, "head", None),
        P("blk", None, "head", None),
        P(),
        P(),
        P("head", None, None),
        P(None, ("blk", "head"), None),
        P(),
    )
    return jax.shard_map(
        shards,
        mesh=mesh,
        in_specs=placed,
        out_specs=P(None, ("blk", "head"), None),
        check_vma=False,
    )
```

```python
import functools

import jax
import jax.numpy as jnp
from jax import lax
from jax.experimental import pallas as pl
from jax.experimental.pallas import tpu as pltpu
from jax.sharding import PartitionSpec as P

soft_cap = 50.0
score_scale = 144.0 ** (-0.5)
norm_eps = 1e-06

MESH_ID = pl.DeviceIdType.MESH


def attend_kernel(
    zs_n,
    tok,
    kv_hbm,
    q_hbm,
    mask_ref,
    out_ref,
    kvbuf,
    qall,
    acc,
    att_send,
    att_recv,
    local_sem,
    send_sem,
    recv_sem,
    x_send,
    x_recv,
):
    blk = lax.axis_index("blk")
    me_c = lax.rem(blk, 2)
    me_z = lax.rem(blk // 2, zs_n)
    me_x = blk // (2 * zs_n)

    def place(x, z, c):
        return {"blk": (x * zs_n + z) * 2 + c}

    right = place(me_x, lax.rem(me_z + 1, zs_n), me_c)
    left = place(me_x, lax.rem(me_z + zs_n - 1, zs_n), me_c)
    sibling = place(me_x, me_z, 1 - me_c)
    partner = place(1 - me_x, me_z, me_c)

    barrier = pltpu.get_barrier_semaphore()
    for other in (right, left, sibling, partner):
        pl.semaphore_signal(barrier, inc=1, device_id=other, device_id_type=MESH_ID)

    own_kv = pltpu.make_async_copy(kv_hbm.at[me_x], kvbuf.at[me_c, me_x, me_z], local_sem.at[0])
    own_q = pltpu.make_async_copy(q_hbm.at[me_x], qall.at[me_x], local_sem.at[1])
    own_kv.start()
    own_q.start()
    pl.semaphore_wait(barrier, 4)

    q_swap = pltpu.make_async_remote_copy(
        src_ref=q_hbm.at[1 - me_x],
        dst_ref=qall.at[me_x],
        send_sem=x_send.at[0],
        recv_sem=x_recv.at[0],
        device_id=partner,
        device_id_type=MESH_ID,
    )
    kv_swap = pltpu.make_async_remote_copy(
        src_ref=kv_hbm.at[1 - me_x],
        dst_ref=kvbuf.at[me_c, me_x, me_z],
        send_sem=x_send.at[1],
        recv_sem=recv_sem.at[me_c, me_x, me_z],
        device_id=partner,
        device_id_type=MESH_ID,
    )
    q_swap.start()
    kv_swap.start()

    def forward(way, device, x, z):
        return pltpu.make_async_remote_copy(
            src_ref=kvbuf.at[me_c, x, z],
            dst_ref=kvbuf.at[me_c, x, z],
            send_sem=send_sem.at[way, x, z],
            recv_sem=recv_sem.at[me_c, x, z],
            device_id=device,
            device_id_type=MESH_ID,
        )

    def landed(c, x, z):
        pltpu.make_async_remote_copy(
            src_ref=kvbuf.at[c, x, z],
            dst_ref=kvbuf.at[c, x, z],
            send_sem=x_send.at[1],
            recv_sem=recv_sem.at[c, x, z],
            device_id=sibling,
            device_id_type=MESH_ID,
        ).wait_recv()

    half = zs_n // 2
    last = zs_n

    def steps_right(k):
        is_b = (lax.rem(k, 2) == 0) & (k > 0)
        dist = jnp.where(lax.rem(k, 2) == 1, (k + 1) // 2, jnp.maximum(k - 2, 0) // 2)
        x = jnp.where(is_b, 1 - me_x, me_x)
        return x, lax.rem(me_z - dist + zs_n, zs_n)

    def steps_left(k):
        is_b = ((lax.rem(k, 2) == 0) & (k > 0)) | (k == last - 1)
        dist = jnp.where(lax.rem(k, 2) == 1, (k + 1) // 2, jnp.maximum(k - 2, 0) // 2)
        dist = jnp.where(k >= last - 1, k - (last - half), dist)
        x = jnp.where(is_b, 1 - me_x, me_x)
        return x, lax.rem(me_z + dist, zs_n)

    def goes_right(k):
        return k <= last - 2

    def goes_left(k):
        return (k != last - 3) & (k != last)

    def is_own(k):
        return (k == 0) | (k == 2)

    rows = 2 * tok
    lane = lax.broadcasted_iota(jnp.int32, (rows, tok), 1)
    row = lax.broadcasted_iota(jnp.int32, (rows, tok), 0)
    ahead = lax.rem(row, tok) - lane

    def weigh(scores):
        capped = jnp.tanh(scores * (score_scale / soft_cap)) * soft_cap
        return jnp.exp(capped)

    ones = jnp.ones((3 * tok, 128), jnp.bfloat16)

    def dots(a, b):
        return lax.dot_general(
            a, b, (((1,), (1,)), ((), ())), preferred_element_type=jnp.float32
        )

    def attend(c, x, z):
        key_block = (x * zs_n + z) * 2 + c
        seen = mask_ref[key_block]
        for r in range(2):
            pool = pl.ds(tok, 2 * tok)
            new = pl.ds(r * 3 * tok, tok)
            every = pl.ds(r * tok, 3 * tok)
            pool_k = kvbuf[c, x, z, 0, pool, :]
            new_k = kvbuf[c, x, z, 0, new, :]
            values = jnp.concatenate([kvbuf[c, x, z, 1, every, :], ones], axis=1)
            for qx in range(2):
                query = qall[qx, r]
                query_block = (qx * zs_n + me_z) * 2 + me_c
                w_pool = weigh(dots(query, pool_k)) * seen[r : r + 1, :]
                w_new = jnp.where(
                    ahead >= (key_block - query_block) * tok, weigh(dots(query, new_k)), 0.0
                )
                both = [w_new, w_pool] if r == 0 else [w_pool, w_new]
                weights = jnp.concatenate(both, axis=1).astype(jnp.bfloat16)
                acc[qx, r] += jnp.dot(weights, values, preferred_element_type=jnp.float32)

    own_kv.wait()
    acc[...] = jnp.zeros_like(acc)

    def one_step(k, carry):
        rx, rz = steps_right(k)
        lx, lz = steps_left(k)
        own = is_own(k)

        @pl.when(k > 0)
        def _():
            landed(me_c, rx, rz)

        @pl.when(goes_right(k))
        def _():
            forward(0, right, rx, rz).start()

        @pl.when(jnp.logical_not(own))
        def _():
            landed(me_c, lx, lz)

        @pl.when(goes_left(k))
        def _():
            forward(1, left, lx, lz).start()

        forward(2, sibling, rx, rz).start()

        @pl.when(jnp.logical_not(own))
        def _():
            forward(2, sibling, lx, lz).start()

        @pl.when(k == 0)
        def _():
            own_q.wait()
            q_swap.wait_recv()

        def one_shard(i, carry):
            c = jnp.where(i % 2 == 0, me_c, 1 - me_c)
            x = jnp.where(i < 2, rx, lx)
            z = jnp.where(i < 2, rz, lz)

            @pl.when(i % 2 == 1)
            def _():
                landed(c, x, z)

            attend(c, x, z)
            return carry

        lax.fori_loop(0, jnp.where(own, 2, 4), one_shard, 0)
        return carry

    lax.fori_loop(0, last + 1, one_step, 0)

    def finished(qx, r):
        total = acc[qx, r]
        return (total[:, :128] / total[:, 128:]).astype(jnp.bfloat16)

    for r in range(2):
        att_send[r] = finished(1 - me_x, r)
    att_swap = pltpu.make_async_remote_copy(
        src_ref=att_send,
        dst_ref=att_recv,
        send_sem=x_send.at[2],
        recv_sem=x_recv.at[1],
        device_id=partner,
        device_id_type=MESH_ID,
    )
    att_swap.start()

    share = tok // 8

    def put(x, r, value):
        for g in range(2):
            columns = pl.ds(pl.multiple_of((2 * x + g) * 128, 128), 128)
            out_ref[:, r, :, columns] = value[g * tok : (g + 1) * tok].reshape(8, share, 128)

    for r in range(2):
        put(me_x, r, finished(me_x, r))
    att_swap.wait()
    for r in range(2):
        put(1 - me_x, r, att_recv[r])

    q_swap.wait_send()
    kv_swap.wait_send()

    def drain(k, carry):
        rx, rz = steps_right(k)
        lx, lz = steps_left(k)

        @pl.when(goes_right(k))
        def _():
            forward(0, right, rx, rz).wait_send()

        @pl.when(goes_left(k))
        def _():
            forward(1, left, lx, lz).wait_send()

        forward(2, sibling, rx, rz).wait_send()

        @pl.when(jnp.logical_not(is_own(k)))
        def _():
            forward(2, sibling, lx, lz).wait_send()

        return carry

    lax.fori_loop(0, last + 1, drain, 0)


def gather_and_attend(queries, new_keys, new_values, pool_keys, pool_values, page_table, cache_len):
    req, tok, heads, dim = queries.shape
    kv_heads = new_keys.shape[2]
    zs_n = lax.axis_size("blk") // 4

    def laid(new, pool):
        new = new.transpose(2, 0, 1, 3)
        pool = pool.transpose(2, 0, 1, 3).reshape(kv_heads, 2 * tok, dim)
        return jnp.concatenate([new[:, 0], pool, new[:, 1]], axis=1)

    kv = jnp.stack([laid(new_keys, pool_keys), laid(new_values, pool_values)], axis=1)
    q = queries.reshape(req, tok, kv_heads, heads // kv_heads, dim)
    q = q.transpose(2, 0, 3, 1, 4).reshape(kv_heads, req, 2 * tok, dim)

    pages = 2 * lax.axis_size("blk")
    slots = page_table.shape[1]
    match = jnp.arange(pages, dtype=jnp.int32)[:, None, None] == page_table[None]
    slot = jnp.sum(jnp.where(match, jnp.arange(slots, dtype=jnp.int32), 0), axis=2)
    owned = jnp.any(match, axis=2)
    position = slot[:, :, None] * tok + jnp.arange(tok, dtype=jnp.int32)
    seen = (owned[:, :, None] & (position < cache_len[None, :, None])).astype(jnp.float32)
    seen = seen.reshape(pages // 2, 2, req, tok).transpose(0, 2, 1, 3)
    seen = seen.reshape(pages // 2, req, 2 * tok)

    hbm = pl.BlockSpec(memory_space=pl.ANY)
    vmem = pl.BlockSpec(memory_space=pltpu.VMEM)
    return pl.pallas_call(
        functools.partial(attend_kernel, zs_n, tok),
        name="gather_and_attend",
        out_shape=jax.ShapeDtypeStruct((8, req, tok // 8, heads * dim), jnp.bfloat16),
        in_specs=[hbm, hbm, vmem],
        out_specs=vmem,
        scratch_shapes=[
            pltpu.VMEM((2, 2, zs_n, 2, 4 * tok, dim), jnp.bfloat16),
            pltpu.VMEM((2, req, 2 * tok, dim), jnp.bfloat16),
            pltpu.VMEM((2, req, 2 * tok, 2 * dim), jnp.float32),
            pltpu.VMEM((req, 2 * tok, dim), jnp.bfloat16),
            pltpu.VMEM((req, 2 * tok, dim), jnp.bfloat16),
            pltpu.SemaphoreType.DMA((2,)),
            pltpu.SemaphoreType.DMA((3, 2, zs_n)),
            pltpu.SemaphoreType.DMA((2, 2, zs_n)),
            pltpu.SemaphoreType.DMA((3,)),
            pltpu.SemaphoreType.DMA((2,)),
        ],
        compiler_params=pltpu.CompilerParams(collective_id=0, has_side_effects=True),
    )(kv, q, seen)


def project_kernel(
    att_ref, weight_hbm, residual_ref, gain_ref, out_ref, weight, part, got, total, w_sem, send_sem, recv_sem
):
    me = lax.axis_index("head")
    me_y, me_h = me // 2, lax.rem(me, 2)
    thirds = 3
    wide = part.shape[2] // thirds
    tile = 512

    def loads(t):
        columns = pl.ds(t * wide, wide)
        return pltpu.make_async_copy(weight_hbm.at[:, columns], weight.at[:, columns], w_sem.at[t])

    for t in range(thirds):
        loads(t).start()

    peers = []
    for dy, dh in ((1, 0), (3, 0), (0, 1), (2, 0), (1, 1), (3, 1), (2, 1)):
        to = lax.rem(me_y + dy, 4) * 2 + lax.rem(me_h + dh, 2)
        source = lax.rem(me_y + 4 - dy, 4) * 2 + lax.rem(me_h + dh, 2)
        peers.append((to, source))

    barrier = pltpu.get_barrier_semaphore()
    for to, _ in peers:
        pl.semaphore_signal(barrier, inc=1, device_id={"head": to}, device_id_type=MESH_ID)

    def sends(i, t):
        columns = pl.ds(t * wide, wide)
        to = peers[i][0]
        return pltpu.make_async_remote_copy(
            src_ref=part.at[to, :, columns],
            dst_ref=got.at[i, :, columns],
            send_sem=send_sem.at[t, i],
            recv_sem=recv_sem.at[t, i],
            device_id={"head": to},
            device_id_type=MESH_ID,
        )

    attended = att_ref[...].reshape(8 * 32, att_ref.shape[3])
    for t in range(thirds):
        loads(t).wait()

        def one_tile(i, carry):
            columns = pl.ds(pl.multiple_of(t * wide + i * tile, tile), tile)
            value = jnp.dot(attended, weight[:, columns], preferred_element_type=jnp.float32)
            part[:, :, columns] = value.astype(jnp.bfloat16).reshape(8, 32, tile)
            return carry

        lax.fori_loop(0, wide // tile, one_tile, 0)
        if t == 0:
            pl.semaphore_wait(barrier, 7)
        for i in range(7):
            sends(i, t).start()

    square = jnp.zeros((32, 1), jnp.float32)
    for t in range(thirds):
        for i in range(7):
            sends(i, t).wait_recv()

        def add_tile(n, square):
            columns = pl.ds(pl.multiple_of(t * wide + n * tile, tile), tile)
            value = part[me, :, columns].astype(jnp.float32)
            for i in range(7):
                value = value + got[i, :, columns].astype(jnp.float32)
            total[:, columns] = value
            return square + jnp.sum(value * value, axis=1, keepdims=True)

        square = lax.fori_loop(0, wide // tile, add_tile, square)

    inv_rms = lax.rsqrt(square / part.shape[2] + norm_eps)

    def mix_tile(n, carry):
        columns = pl.ds(pl.multiple_of(n * tile, tile), tile)
        value = gain_ref[:, columns] * total[:, columns] * inv_rms
        for r in range(2):
            rows = value[r * 16 : (r + 1) * 16]
            out_ref[r, :, columns] = (residual_ref[r, :, columns].astype(jnp.float32) + rows).astype(
                jnp.bfloat16
            )
        return carry

    lax.fori_loop(0, part.shape[2] // tile, mix_tile, 0)
    for t in range(thirds):
        for i in range(7):
            sends(i, t).wait_send()


def project_and_mix(attended, weight_rows, residual, post_gain):
    depth, width = weight_rows.shape
    vmem = pl.BlockSpec(memory_space=pltpu.VMEM)
    return pl.pallas_call(
        project_kernel,
        name="project_and_mix",
        out_shape=jax.ShapeDtypeStruct(residual.shape, jnp.bfloat16),
        in_specs=[vmem, pl.BlockSpec(memory_space=pl.ANY), vmem, vmem],
        out_specs=vmem,
        scratch_shapes=[
            pltpu.VMEM((depth, width), jnp.bfloat16),
            pltpu.VMEM((8, 32, width), jnp.bfloat16),
            pltpu.VMEM((7, 32, width), jnp.bfloat16),
            pltpu.VMEM((32, width), jnp.float32),
            pltpu.SemaphoreType.DMA((3,)),
            pltpu.SemaphoreType.DMA((3, 7)),
            pltpu.SemaphoreType.DMA((3, 7)),
        ],
        compiler_params=pltpu.CompilerParams(collective_id=1, has_side_effects=True),
    )(attended, weight_rows, residual, post_gain.reshape(1, width))


def shards(
    queries,
    new_keys,
    new_values,
    pool_keys,
    pool_values,
    page_table,
    cache_len,
    out_weight,
    residual,
    post_gain,
):
    heads, dim, width = out_weight.shape
    attended = gather_and_attend(
        queries, new_keys, new_values, pool_keys, pool_values, page_table, cache_len
    )
    return project_and_mix(attended, out_weight.reshape(heads * dim, width), residual, post_gain)


def solution(mesh):
    placed = (
        P(None, "blk", "head", None),
        P(None, "blk", "head", None),
        P(None, "blk", "head", None),
        P("blk", None, "head", None),
        P("blk", None, "head", None),
        P(),
        P(),
        P("head", None, None),
        P(None, ("blk", "head"), None),
        P(),
    )
    return jax.shard_map(
        shards,
        mesh=mesh,
        in_specs=placed,
        out_specs=P(None, ("blk", "head"), None),
        check_vma=False,
    )
```

```python
import functools

import jax
import jax.numpy as jnp
from jax import lax
from jax.experimental import pallas as pl
from jax.experimental.pallas import tpu as pltpu
from jax.sharding import PartitionSpec as P

soft_cap = 50.0
score_scale = 144.0 ** (-0.5)
norm_eps = 1e-06
log2_e = 1.4426950408889634

MESH_ID = pl.DeviceIdType.MESH


def attend_kernel(
    zs_n,
    tok,
    kv_hbm,
    q_hbm,
    table_ref,
    length_ref,
    out_ref,
    kvbuf,
    qall,
    acc,
    seen,
    first,
    att_send,
    att_recv,
    local_sem,
    send_sem,
    recv_sem,
    x_send,
    x_recv,
):
    blk = lax.axis_index("blk")
    me_c = lax.rem(blk, 2)
    me_z = lax.rem(blk // 2, zs_n)
    me_x = blk // (2 * zs_n)

    def place(x, z, c):
        return {"blk": (x * zs_n + z) * 2 + c}

    right = place(me_x, lax.rem(me_z + 1, zs_n), me_c)
    left = place(me_x, lax.rem(me_z + zs_n - 1, zs_n), me_c)
    sibling = place(me_x, me_z, 1 - me_c)
    partner = place(1 - me_x, me_z, me_c)

    barrier = pltpu.get_barrier_semaphore()
    for other in (right, left, sibling, partner):
        pl.semaphore_signal(barrier, inc=1, device_id=other, device_id_type=MESH_ID)

    own_kv = pltpu.make_async_copy(kv_hbm.at[me_x], kvbuf.at[me_c, me_x, me_z], local_sem.at[0])
    own_q = pltpu.make_async_copy(q_hbm.at[me_x], qall.at[me_x], local_sem.at[1])
    own_kv.start()
    own_q.start()
    pl.semaphore_wait(barrier, 4)

    q_swap = pltpu.make_async_remote_copy(
        src_ref=q_hbm.at[1 - me_x],
        dst_ref=qall.at[me_x],
        send_sem=x_send.at[0],
        recv_sem=x_recv.at[0],
        device_id=partner,
        device_id_type=MESH_ID,
    )

    def kv_swap(h):
        return pltpu.make_async_remote_copy(
            src_ref=kv_hbm.at[1 - me_x, h],
            dst_ref=kvbuf.at[me_c, me_x, me_z, h],
            send_sem=x_send.at[2 + h],
            recv_sem=x_recv.at[2 + h],
            device_id=partner,
            device_id_type=MESH_ID,
        )

    def kv_swap_landed(h):
        here = kvbuf.at[me_c, 1 - me_x, me_z, h]
        pltpu.make_async_remote_copy(
            src_ref=here,
            dst_ref=here,
            send_sem=x_send.at[2 + h],
            recv_sem=x_recv.at[2 + h],
            device_id=partner,
            device_id_type=MESH_ID,
        ).wait_recv()

    q_swap.start()
    kv_swap(0).start()
    kv_swap(1).start()

    def forward(way, device, x, z):
        return pltpu.make_async_remote_copy(
            src_ref=kvbuf.at[me_c, x, z],
            dst_ref=kvbuf.at[me_c, x, z],
            send_sem=send_sem.at[way, x, z],
            recv_sem=recv_sem.at[me_c, x, z],
            device_id=device,
            device_id_type=MESH_ID,
        )

    def forward_half(way, device, x, z, h):
        return pltpu.make_async_remote_copy(
            src_ref=kvbuf.at[me_c, x, z, h],
            dst_ref=kvbuf.at[me_c, x, z, h],
            send_sem=send_sem.at[way, x, z],
            recv_sem=recv_sem.at[me_c, x, z],
            device_id=device,
            device_id_type=MESH_ID,
        )

    def landed(c, x, z):
        pltpu.make_async_remote_copy(
            src_ref=kvbuf.at[c, x, z],
            dst_ref=kvbuf.at[c, x, z],
            send_sem=x_send.at[1],
            recv_sem=recv_sem.at[c, x, z],
            device_id=sibling,
            device_id_type=MESH_ID,
        ).wait_recv()

    last = zs_n

    def steps_right(k):
        x = jnp.where(lax.rem(k, 2) == 1, 1 - me_x, me_x)
        return x, lax.rem(me_z - k // 2 + zs_n, zs_n)

    def steps_left(k):
        x = jnp.where((lax.rem(k, 2) == 1) | (k == last), 1 - me_x, me_x)
        return x, lax.rem(me_z + k // 2, zs_n)

    def goes_right(k):
        return k <= last - 2

    def goes_left(k):
        return (k != last - 2) & (k != last)

    own_kv.wait()
    forward(0, right, me_x, me_z).start()
    forward(1, left, me_x, me_z).start()
    forward(2, sibling, me_x, me_z).start()

    pages, slots = first.shape[0], table_ref.shape[1]
    page_id = lax.broadcasted_iota(jnp.int32, (pages, slots), 0)
    slot_id = lax.broadcasted_iota(jnp.int32, (pages, slots), 1).astype(jnp.float32)
    offset = lax.broadcasted_iota(jnp.int32, (pages, tok), 1)
    for r in range(2):
        match = page_id == table_ref[r : r + 1, :]
        slot = jnp.sum(jnp.where(match, slot_id, 0.0), axis=1, keepdims=True).astype(jnp.int32)
        owned = jnp.sum(jnp.where(match, 1.0, 0.0), axis=1, keepdims=True)
        visible = slot * tok + offset < length_ref[r]
        seen[r] = jnp.where(visible, owned, 0.0)
        if r == 0:
            first[...] = jnp.broadcast_to(owned, (pages, tok))
    acc[...] = jnp.zeros_like(acc)

    rows = 2 * tok
    lane = lax.broadcasted_iota(jnp.int32, (rows, tok), 1)
    row = lax.broadcasted_iota(jnp.int32, (rows, tok), 0)
    ahead = lax.rem(row, tok) - lane

    def weigh(scores):
        capped = jnp.tanh(scores * (score_scale / soft_cap))
        return jnp.exp2(capped * (soft_cap * log2_e))

    ones = jnp.ones((3 * tok, 128), jnp.bfloat16)

    def dots(a, b):
        return lax.dot_general(
            a, b, (((1,), (1,)), ((), ())), preferred_element_type=jnp.float32
        )

    def attend(c, x, z, which):
        key_block = (x * zs_n + z) * 2 + c
        for qx in which:
            query_block = (qx * zs_n + me_z) * 2 + me_c
            w_page = []
            for p in range(2):
                pick = first[pl.ds(2 * key_block + p, 1), :].astype(jnp.bfloat16)
                query = qall[qx, 0] * pick + qall[qx, 1] * (1 - pick)
                w_page.append(weigh(dots(query, kvbuf[c, x, z, 0, pl.ds((1 + p) * tok, tok), :])))
            for r in range(2):
                w_new = jnp.where(
                    ahead >= (key_block - query_block) * tok,
                    weigh(dots(qall[qx, r], kvbuf[c, x, z, 0, pl.ds(r * 3 * tok, tok), :])),
                    0.0,
                )
                w_pool = [w_page[p] * seen[r, pl.ds(2 * key_block + p, 1), :] for p in range(2)]
                both = [w_new] + w_pool if r == 0 else w_pool + [w_new]
                weights = jnp.concatenate(both, axis=1).astype(jnp.bfloat16)
                values = jnp.concatenate(
                    [kvbuf[c, x, z, 1, pl.ds(r * tok, 3 * tok), :], ones], axis=1
                )
                acc[qx, r] += jnp.dot(weights, values, preferred_element_type=jnp.float32)

    own_q.wait()
    q_swap.wait_recv()

    def receive(k):
        rx, rz = steps_right(k)
        lx, lz = steps_left(k)
        landed(me_c, rx, rz)

        @pl.when(goes_right(k))
        def _():
            forward(0, right, rx, rz).start()

        landed(me_c, lx, lz)

        @pl.when(goes_left(k))
        def _():
            forward(1, left, lx, lz).start()

        forward(2, sibling, rx, rz).start()
        forward(2, sibling, lx, lz).start()

    def one_step(k, carry):
        rx, rz = steps_right(k)
        lx, lz = steps_left(k)
        own = k <= 1

        @pl.when(k == 1)
        def _():
            for h in range(2):
                kv_swap_landed(h)
                forward_half(0, right, rx, rz, h).start()
                forward_half(1, left, rx, rz, h).start()
            forward(2, sibling, rx, rz).start()

        @pl.when(k > 1)
        def _():
            receive(k)

        def one_shard(i, carry):
            mine = jnp.where(own, 1, 2) > i
            c = jnp.where(mine, me_c, 1 - me_c)
            from_left = own | (lax.rem(i, 2) == 0)
            x = jnp.where(from_left, rx, lx)
            z = jnp.where(from_left, rz, lz)

            @pl.when(jnp.logical_not(mine))
            def _():
                landed(c, x, z)

            attend(c, x, z, (0, 1))
            return carry

        lax.fori_loop(0, jnp.where(own, 2, 4), one_shard, 0)
        return carry

    lax.fori_loop(0, last, one_step, 0)

    def finished(qx, r):
        total = acc[qx, r]
        return (total[:, :128] / total[:, 128:]).astype(jnp.bfloat16)

    att_swap = pltpu.make_async_remote_copy(
        src_ref=att_send,
        dst_ref=att_recv,
        send_sem=x_send.at[1],
        recv_sem=x_recv.at[1],
        device_id=partner,
        device_id_type=MESH_ID,
    )

    receive(last)
    end_rx, end_rz = steps_right(last)
    end_lx, end_lz = steps_left(last)

    def end_shard(i, carry):
        mine = lax.rem(i, 4) < 2
        c = jnp.where(mine, me_c, 1 - me_c)
        from_left = lax.rem(i, 2) == 0
        x = jnp.where(from_left, end_rx, end_lx)
        z = jnp.where(from_left, end_rz, end_lz)

        @pl.when((i == 2) | (i == 3))
        def _():
            landed(c, x, z)

        attend(c, x, z, (jnp.where(i < 4, 1 - me_x, me_x),))

        @pl.when(i == 3)
        def _():
            for r in range(2):
                att_send[r] = finished(1 - me_x, r)
            att_swap.start()

        return carry

    lax.fori_loop(0, 8, end_shard, 0)

    share = tok // 8

    def put(x, r, value):
        for g in range(2):
            columns = pl.ds(pl.multiple_of((2 * x + g) * 128, 128), 128)
            out_ref[:, r, :, columns] = value[g * tok : (g + 1) * tok].reshape(8, share, 128)

    for r in range(2):
        put(me_x, r, finished(me_x, r))
    att_swap.wait()
    for r in range(2):
        put(1 - me_x, r, att_recv[r])

    q_swap.wait_send()
    kv_swap(0).wait_send()
    kv_swap(1).wait_send()

    def drain(k, carry):
        rx, rz = steps_right(k)
        lx, lz = steps_left(k)

        @pl.when(goes_right(k))
        def _():
            forward(0, right, rx, rz).wait_send()

        @pl.when(goes_left(k))
        def _():
            forward(1, left, lx, lz).wait_send()

        forward(2, sibling, rx, rz).wait_send()

        @pl.when(k > 1)
        def _():
            forward(2, sibling, lx, lz).wait_send()

        return carry

    lax.fori_loop(0, last + 1, drain, 0)


def gather_and_attend(queries, new_keys, new_values, pool_keys, pool_values, page_table, cache_len):
    req, tok, heads, dim = queries.shape
    kv_heads = new_keys.shape[2]
    zs_n = lax.axis_size("blk") // 4

    def laid(new, pool):
        new = new.transpose(2, 0, 1, 3)
        pool = pool.transpose(2, 0, 1, 3).reshape(kv_heads, 2 * tok, dim)
        return jnp.concatenate([new[:, 0], pool, new[:, 1]], axis=1)

    kv = jnp.stack([laid(new_keys, pool_keys), laid(new_values, pool_values)], axis=1)
    q = queries.reshape(req, tok, kv_heads, heads // kv_heads, dim)
    q = q.transpose(2, 0, 3, 1, 4).reshape(kv_heads, req, 2 * tok, dim)

    pages = 2 * lax.axis_size("blk")

    hbm = pl.BlockSpec(memory_space=pl.ANY)
    vmem = pl.BlockSpec(memory_space=pltpu.VMEM)
    return pl.pallas_call(
        functools.partial(attend_kernel, zs_n, tok),
        name="gather_and_attend",
        out_shape=jax.ShapeDtypeStruct((8, req, tok // 8, heads * dim), jnp.bfloat16),
        in_specs=[hbm, hbm, vmem, pl.BlockSpec(memory_space=pltpu.SMEM)],
        out_specs=vmem,
        scratch_shapes=[
            pltpu.VMEM((2, 2, zs_n, 2, 4 * tok, dim), jnp.bfloat16),
            pltpu.VMEM((2, req, 2 * tok, dim), jnp.bfloat16),
            pltpu.VMEM((2, req, 2 * tok, 2 * dim), jnp.float32),
            pltpu.VMEM((req, pages, tok), jnp.float32),
            pltpu.VMEM((pages, tok), jnp.float32),
            pltpu.VMEM((req, 2 * tok, dim), jnp.bfloat16),
            pltpu.VMEM((req, 2 * tok, dim), jnp.bfloat16),
            pltpu.SemaphoreType.DMA((2,)),
            pltpu.SemaphoreType.DMA((3, 2, zs_n)),
            pltpu.SemaphoreType.DMA((2, 2, zs_n)),
            pltpu.SemaphoreType.DMA((4,)),
            pltpu.SemaphoreType.DMA((4,)),
        ],
        compiler_params=pltpu.CompilerParams(collective_id=0, has_side_effects=True),
    )(kv, q, page_table, cache_len)


def project_kernel(
    att_ref, weight_hbm, residual_ref, gain_ref, out_ref, weight, part, got, total, w_sem, send_sem, recv_sem
):
    me = lax.axis_index("head")
    me_y, me_h = me // 2, lax.rem(me, 2)
    thirds = 3
    wide = part.shape[2] // thirds
    tile = 512

    def loads(t):
        columns = pl.ds(t * wide, wide)
        return pltpu.make_async_copy(weight_hbm.at[:, columns], weight.at[:, columns], w_sem.at[t])

    for t in range(thirds):
        loads(t).start()

    peers = []
    for dy, dh in ((1, 0), (3, 0), (0, 1), (2, 0), (1, 1), (3, 1), (2, 1)):
        to = lax.rem(me_y + dy, 4) * 2 + lax.rem(me_h + dh, 2)
        source = lax.rem(me_y + 4 - dy, 4) * 2 + lax.rem(me_h + dh, 2)
        peers.append((to, source))

    barrier = pltpu.get_barrier_semaphore()
    for to, _ in peers:
        pl.semaphore_signal(barrier, inc=1, device_id={"head": to}, device_id_type=MESH_ID)

    def sends(i, t):
        columns = pl.ds(t * wide, wide)
        to = peers[i][0]
        return pltpu.make_async_remote_copy(
            src_ref=part.at[to, :, columns],
            dst_ref=got.at[i, :, columns],
            send_sem=send_sem.at[t, i],
            recv_sem=recv_sem.at[t, i],
            device_id={"head": to},
            device_id_type=MESH_ID,
        )

    attended = att_ref[...].reshape(8 * 32, att_ref.shape[3])
    for t in range(thirds):
        loads(t).wait()

        def one_tile(i, carry):
            columns = pl.ds(pl.multiple_of(t * wide + i * tile, tile), tile)
            value = jnp.dot(attended, weight[:, columns], preferred_element_type=jnp.float32)
            part[:, :, columns] = value.astype(jnp.bfloat16).reshape(8, 32, tile)
            return carry

        lax.fori_loop(0, wide // tile, one_tile, 0)
        if t == 0:
            pl.semaphore_wait(barrier, 7)
        for i in range(7):
            sends(i, t).start()

    square = jnp.zeros((32, 1), jnp.float32)
    for t in range(thirds):
        for i in range(7):
            sends(i, t).wait_recv()

        def add_tile(n, square):
            columns = pl.ds(pl.multiple_of(t * wide + n * tile, tile), tile)
            value = part[me, :, columns].astype(jnp.float32)
            for i in range(7):
                value = value + got[i, :, columns].astype(jnp.float32)
            total[:, columns] = value
            return square + jnp.sum(value * value, axis=1, keepdims=True)

        square = lax.fori_loop(0, wide // tile, add_tile, square)

    inv_rms = lax.rsqrt(square / part.shape[2] + norm_eps)

    def mix_tile(n, carry):
        columns = pl.ds(pl.multiple_of(n * tile, tile), tile)
        value = gain_ref[:, columns] * total[:, columns] * inv_rms
        for r in range(2):
            rows = value[r * 16 : (r + 1) * 16]
            out_ref[r, :, columns] = (residual_ref[r, :, columns].astype(jnp.float32) + rows).astype(
                jnp.bfloat16
            )
        return carry

    lax.fori_loop(0, part.shape[2] // tile, mix_tile, 0)
    for t in range(thirds):
        for i in range(7):
            sends(i, t).wait_send()


def project_and_mix(attended, weight_rows, residual, post_gain):
    depth, width = weight_rows.shape
    vmem = pl.BlockSpec(memory_space=pltpu.VMEM)
    return pl.pallas_call(
        project_kernel,
        name="project_and_mix",
        out_shape=jax.ShapeDtypeStruct(residual.shape, jnp.bfloat16),
        in_specs=[vmem, pl.BlockSpec(memory_space=pl.ANY), vmem, vmem],
        out_specs=vmem,
        scratch_shapes=[
            pltpu.VMEM((depth, width), jnp.bfloat16),
            pltpu.VMEM((8, 32, width), jnp.bfloat16),
            pltpu.VMEM((7, 32, width), jnp.bfloat16),
            pltpu.VMEM((32, width), jnp.float32),
            pltpu.SemaphoreType.DMA((3,)),
            pltpu.SemaphoreType.DMA((3, 7)),
            pltpu.SemaphoreType.DMA((3, 7)),
        ],
        compiler_params=pltpu.CompilerParams(collective_id=1, has_side_effects=True),
    )(attended, weight_rows, residual, post_gain.reshape(1, width))


def shards(
    queries,
    new_keys,
    new_values,
    pool_keys,
    pool_values,
    page_table,
    cache_len,
    out_weight,
    residual,
    post_gain,
):
    heads, dim, width = out_weight.shape
    attended = gather_and_attend(
        queries, new_keys, new_values, pool_keys, pool_values, page_table, cache_len
    )
    return project_and_mix(attended, out_weight.reshape(heads * dim, width), residual, post_gain)


def solution(mesh):
    placed = (
        P(None, "blk", "head", None),
        P(None, "blk", "head", None),
        P(None, "blk", "head", None),
        P("blk", None, "head", None),
        P("blk", None, "head", None),
        P(),
        P(),
        P("head", None, None),
        P(None, ("blk", "head"), None),
        P(),
    )
    return jax.shard_map(
        shards,
        mesh=mesh,
        in_specs=placed,
        out_specs=P(None, ("blk", "head"), None),
        check_vma=False,
    )
```

```python
import functools

import jax
import jax.numpy as jnp
from jax import lax
from jax.experimental import pallas as pl
from jax.experimental.pallas import tpu as pltpu
from jax.sharding import PartitionSpec as P

soft_cap = 50.0
score_scale = 144.0 ** (-0.5)
norm_eps = 1e-06
log2_e = 1.4426950408889634

MESH_ID = pl.DeviceIdType.MESH


def attend_kernel(
    zs_n,
    tok,
    kv_hbm,
    q_hbm,
    table_ref,
    length_ref,
    out_ref,
    kvbuf,
    qall,
    acc,
    seen,
    first,
    att_send,
    att_recv,
    local_sem,
    send_sem,
    recv_sem,
    x_send,
    x_recv,
):
    blk = lax.axis_index("blk")
    me_c = lax.rem(blk, 2)
    me_z = lax.rem(blk // 2, zs_n)
    me_x = blk // (2 * zs_n)

    def place(x, z, c):
        return {"blk": (x * zs_n + z) * 2 + c}

    right = place(me_x, lax.rem(me_z + 1, zs_n), me_c)
    left = place(me_x, lax.rem(me_z + zs_n - 1, zs_n), me_c)
    sibling = place(me_x, me_z, 1 - me_c)
    partner = place(1 - me_x, me_z, me_c)

    barrier = pltpu.get_barrier_semaphore()
    for other in (right, left, sibling, partner):
        pl.semaphore_signal(barrier, inc=1, device_id=other, device_id_type=MESH_ID)

    own_kv = pltpu.make_async_copy(kv_hbm.at[me_x], kvbuf.at[me_c, me_x, me_z], local_sem.at[0])
    own_q = pltpu.make_async_copy(q_hbm.at[me_x], qall.at[me_x], local_sem.at[1])
    own_kv.start()
    own_q.start()
    pl.semaphore_wait(barrier, 4)

    q_swap = pltpu.make_async_remote_copy(
        src_ref=q_hbm.at[1 - me_x],
        dst_ref=qall.at[me_x],
        send_sem=x_send.at[0],
        recv_sem=x_recv.at[0],
        device_id=partner,
        device_id_type=MESH_ID,
    )

    def kv_swap(h):
        return pltpu.make_async_remote_copy(
            src_ref=kv_hbm.at[1 - me_x, h],
            dst_ref=kvbuf.at[me_c, me_x, me_z, h],
            send_sem=x_send.at[2 + h],
            recv_sem=x_recv.at[2 + h],
            device_id=partner,
            device_id_type=MESH_ID,
        )

    def kv_swap_landed(h):
        here = kvbuf.at[me_c, 1 - me_x, me_z, h]
        pltpu.make_async_remote_copy(
            src_ref=here,
            dst_ref=here,
            send_sem=x_send.at[2 + h],
            recv_sem=x_recv.at[2 + h],
            device_id=partner,
            device_id_type=MESH_ID,
        ).wait_recv()

    q_swap.start()
    kv_swap(0).start()
    kv_swap(1).start()

    def forward(way, device, x, z):
        return pltpu.make_async_remote_copy(
            src_ref=kvbuf.at[me_c, x, z],
            dst_ref=kvbuf.at[me_c, x, z],
            send_sem=send_sem.at[way, x, z],
            recv_sem=recv_sem.at[me_c, x, z],
            device_id=device,
            device_id_type=MESH_ID,
        )

    def forward_half(way, device, x, z, h):
        return pltpu.make_async_remote_copy(
            src_ref=kvbuf.at[me_c, x, z, h],
            dst_ref=kvbuf.at[me_c, x, z, h],
            send_sem=send_sem.at[way, x, z],
            recv_sem=recv_sem.at[me_c, x, z],
            device_id=device,
            device_id_type=MESH_ID,
        )

    def first_sends():
        for way, device in ((0, right), (1, left), (2, sibling)):
            pltpu.make_async_remote_copy(
                src_ref=kv_hbm.at[me_x],
                dst_ref=kvbuf.at[me_c, me_x, me_z],
                send_sem=send_sem.at[way, me_x, me_z],
                recv_sem=recv_sem.at[me_c, me_x, me_z],
                device_id=device,
                device_id_type=MESH_ID,
            ).start()

    first_sends()

    def landed(c, x, z):
        pltpu.make_async_remote_copy(
            src_ref=kvbuf.at[c, x, z],
            dst_ref=kvbuf.at[c, x, z],
            send_sem=x_send.at[1],
            recv_sem=recv_sem.at[c, x, z],
            device_id=sibling,
            device_id_type=MESH_ID,
        ).wait_recv()

    last = zs_n

    def steps_right(k):
        x = jnp.where(lax.rem(k, 2) == 1, 1 - me_x, me_x)
        return x, lax.rem(me_z - k // 2 + zs_n, zs_n)

    def steps_left(k):
        x = jnp.where((lax.rem(k, 2) == 1) | (k == last), 1 - me_x, me_x)
        return x, lax.rem(me_z + k // 2, zs_n)

    def goes_right(k):
        return k <= last - 2

    def goes_left(k):
        return (k != last - 2) & (k != last)


    pages, slots = first.shape[0], table_ref.shape[1]
    page_id = lax.broadcasted_iota(jnp.int32, (pages, slots), 0)
    slot_id = lax.broadcasted_iota(jnp.int32, (pages, slots), 1).astype(jnp.float32)
    offset = lax.broadcasted_iota(jnp.int32, (pages, tok), 1)
    for r in range(2):
        match = page_id == table_ref[r : r + 1, :]
        slot = jnp.sum(jnp.where(match, slot_id, 0.0), axis=1, keepdims=True).astype(jnp.int32)
        owned = jnp.sum(jnp.where(match, 1.0, 0.0), axis=1, keepdims=True)
        visible = slot * tok + offset < length_ref[r]
        seen[r] = jnp.where(visible, owned, 0.0)
        if r == 0:
            first[...] = jnp.broadcast_to(owned, (pages, tok))
    acc[...] = jnp.zeros_like(acc)

    rows = 2 * tok
    lane = lax.broadcasted_iota(jnp.int32, (rows, tok), 1)
    row = lax.broadcasted_iota(jnp.int32, (rows, tok), 0)
    ahead = lax.rem(row, tok) - lane

    def weigh(scores):
        capped = jnp.tanh(scores * (score_scale / soft_cap))
        return jnp.exp2(capped * (soft_cap * log2_e))

    ones = jnp.ones((3 * tok, 128), jnp.bfloat16)

    def dots(a, b):
        return lax.dot_general(
            a, b, (((1,), (1,)), ((), ())), preferred_element_type=jnp.float32
        )

    def attend(c, x, z, which):
        key_block = (x * zs_n + z) * 2 + c
        for qx in which:
            query_block = (qx * zs_n + me_z) * 2 + me_c
            w_page = []
            for p in range(2):
                pick = first[pl.ds(2 * key_block + p, 1), :].astype(jnp.bfloat16)
                query = qall[qx, 0] * pick + qall[qx, 1] * (1 - pick)
                w_page.append(weigh(dots(query, kvbuf[c, x, z, 0, pl.ds((1 + p) * tok, tok), :])))
            for r in range(2):
                w_new = jnp.where(
                    ahead >= (key_block - query_block) * tok,
                    weigh(dots(qall[qx, r], kvbuf[c, x, z, 0, pl.ds(r * 3 * tok, tok), :])),
                    0.0,
                )
                w_pool = [w_page[p] * seen[r, pl.ds(2 * key_block + p, 1), :] for p in range(2)]
                both = [w_new] + w_pool if r == 0 else w_pool + [w_new]
                weights = jnp.concatenate(both, axis=1).astype(jnp.bfloat16)
                values = jnp.concatenate(
                    [kvbuf[c, x, z, 1, pl.ds(r * tok, 3 * tok), :], ones], axis=1
                )
                acc[qx, r] += jnp.dot(weights, values, preferred_element_type=jnp.float32)

    own_kv.wait()
    own_q.wait()
    q_swap.wait_recv()

    def receive(k):
        rx, rz = steps_right(k)
        lx, lz = steps_left(k)
        landed(me_c, rx, rz)

        @pl.when(goes_right(k))
        def _():
            forward(0, right, rx, rz).start()

        landed(me_c, lx, lz)

        @pl.when(goes_left(k))
        def _():
            forward(1, left, lx, lz).start()

        forward(2, sibling, rx, rz).start()
        forward(2, sibling, lx, lz).start()

    def one_step(k, carry):
        rx, rz = steps_right(k)
        lx, lz = steps_left(k)
        own = k <= 1

        @pl.when(k == 1)
        def _():
            for h in range(2):
                kv_swap_landed(h)
                forward_half(0, right, rx, rz, h).start()
                forward_half(1, left, rx, rz, h).start()
            forward(2, sibling, rx, rz).start()

        @pl.when(k > 1)
        def _():
            receive(k)

        def one_shard(i, carry):
            mine = jnp.where(own, 1, 2) > i
            c = jnp.where(mine, me_c, 1 - me_c)
            from_left = own | (lax.rem(i, 2) == 0)
            x = jnp.where(from_left, rx, lx)
            z = jnp.where(from_left, rz, lz)

            @pl.when(jnp.logical_not(mine))
            def _():
                landed(c, x, z)

            attend(c, x, z, (0, 1))
            return carry

        lax.fori_loop(0, jnp.where(own, 2, 4), one_shard, 0)
        return carry

    lax.fori_loop(0, last, one_step, 0)

    def finished(qx, r):
        total = acc[qx, r]
        return (total[:, :128] / total[:, 128:]).astype(jnp.bfloat16)

    att_swap = pltpu.make_async_remote_copy(
        src_ref=att_send,
        dst_ref=att_recv,
        send_sem=x_send.at[1],
        recv_sem=x_recv.at[1],
        device_id=partner,
        device_id_type=MESH_ID,
    )

    receive(last)
    end_rx, end_rz = steps_right(last)
    end_lx, end_lz = steps_left(last)

    def end_shard(i, carry):
        mine = lax.rem(i, 4) < 2
        c = jnp.where(mine, me_c, 1 - me_c)
        from_left = lax.rem(i, 2) == 0
        x = jnp.where(from_left, end_rx, end_lx)
        z = jnp.where(from_left, end_rz, end_lz)

        @pl.when((i == 2) | (i == 3))
        def _():
            landed(c, x, z)

        attend(c, x, z, (jnp.where(i < 4, 1 - me_x, me_x),))

        @pl.when(i == 3)
        def _():
            for r in range(2):
                att_send[r] = finished(1 - me_x, r)
            att_swap.start()

        return carry

    lax.fori_loop(0, 8, end_shard, 0)

    share = tok // 8

    def put(x, r, value):
        for g in range(2):
            columns = pl.ds(pl.multiple_of((2 * x + g) * 128, 128), 128)
            out_ref[:, r, :, columns] = value[g * tok : (g + 1) * tok].reshape(8, share, 128)

    for r in range(2):
        put(me_x, r, finished(me_x, r))
    att_swap.wait()
    for r in range(2):
        put(1 - me_x, r, att_recv[r])

    q_swap.wait_send()
    kv_swap(0).wait_send()
    kv_swap(1).wait_send()

    def drain(k, carry):
        rx, rz = steps_right(k)
        lx, lz = steps_left(k)

        @pl.when(goes_right(k))
        def _():
            forward(0, right, rx, rz).wait_send()

        @pl.when(goes_left(k))
        def _():
            forward(1, left, lx, lz).wait_send()

        forward(2, sibling, rx, rz).wait_send()

        @pl.when(k > 1)
        def _():
            forward(2, sibling, lx, lz).wait_send()

        return carry

    lax.fori_loop(0, last + 1, drain, 0)


def lay_out_kernel(q_ref, nk_ref, nv_ref, pk_ref, pv_ref, kv_ref, q_out):
    def by_head(ref, i, heads):
        rows = ref.shape[1]
        tok = rows // heads
        row = lax.broadcasted_iota(jnp.int32, (rows, rows), 0)
        column = lax.broadcasted_iota(jnp.int32, (rows, rows), 1)
        source = lax.rem(row, tok) * heads + row // tok
        order = jnp.where(source == column, 1.0, 0.0).astype(jnp.bfloat16)
        moved = jnp.dot(order, ref[i], preferred_element_type=jnp.float32)
        return moved.astype(jnp.bfloat16)

    tok = nk_ref.shape[1] // 2
    for n, (new, pool) in enumerate(((nk_ref, pk_ref), (nv_ref, pv_ref))):
        for ref, i, at in ((new, 0, 0), (pool, 0, 1), (pool, 1, 2), (new, 1, 3)):
            moved = by_head(ref, i, 2)
            for k in range(2):
                kv_ref[k, n, at * tok : (at + 1) * tok] = moved[k * tok : (k + 1) * tok]
    for r in range(2):
        moved = by_head(q_ref, r, 4)
        for k in range(2):
            q_out[k, r] = moved[2 * k * tok : 2 * (k + 1) * tok]


def lay_out(queries, new_keys, new_values, pool_keys, pool_values):
    req, tok, heads, dim = queries.shape
    rows = [a.reshape(2, -1, dim) for a in (queries, new_keys, new_values, pool_keys, pool_values)]
    vmem = pl.BlockSpec(memory_space=pltpu.VMEM)
    return pl.pallas_call(
        lay_out_kernel,
        name="lay_out",
        out_shape=(
            jax.ShapeDtypeStruct((2, 2, 4 * tok, dim), jnp.bfloat16),
            jax.ShapeDtypeStruct((2, req, 2 * tok, dim), jnp.bfloat16),
        ),
        in_specs=[vmem] * 5,
        out_specs=(vmem, vmem),
    )(*rows)


def gather_and_attend(queries, new_keys, new_values, pool_keys, pool_values, page_table, cache_len):
    req, tok, heads, dim = queries.shape
    zs_n = lax.axis_size("blk") // 4
    kv, q = lay_out(queries, new_keys, new_values, pool_keys, pool_values)
    pages = 2 * lax.axis_size("blk")

    hbm = pl.BlockSpec(memory_space=pl.ANY)
    vmem = pl.BlockSpec(memory_space=pltpu.VMEM)
    return pl.pallas_call(
        functools.partial(attend_kernel, zs_n, tok),
        name="gather_and_attend",
        out_shape=jax.ShapeDtypeStruct((8, req, tok // 8, heads * dim), jnp.bfloat16),
        in_specs=[hbm, hbm, vmem, pl.BlockSpec(memory_space=pltpu.SMEM)],
        out_specs=vmem,
        scratch_shapes=[
            pltpu.VMEM((2, 2, zs_n, 2, 4 * tok, dim), jnp.bfloat16),
            pltpu.VMEM((2, req, 2 * tok, dim), jnp.bfloat16),
            pltpu.VMEM((2, req, 2 * tok, 2 * dim), jnp.float32),
            pltpu.VMEM((req, pages, tok), jnp.float32),
            pltpu.VMEM((pages, tok), jnp.float32),
            pltpu.VMEM((req, 2 * tok, dim), jnp.bfloat16),
            pltpu.VMEM((req, 2 * tok, dim), jnp.bfloat16),
            pltpu.SemaphoreType.DMA((2,)),
            pltpu.SemaphoreType.DMA((3, 2, zs_n)),
            pltpu.SemaphoreType.DMA((2, 2, zs_n)),
            pltpu.SemaphoreType.DMA((4,)),
            pltpu.SemaphoreType.DMA((4,)),
        ],
        compiler_params=pltpu.CompilerParams(collective_id=0, has_side_effects=True),
    )(kv, q, page_table, cache_len)


def project_kernel(
    att_ref, weight_hbm, residual_ref, gain_ref, out_ref, weight, part, got, total, w_sem, send_sem, recv_sem
):
    me = lax.axis_index("head")
    me_y, me_h = me // 2, lax.rem(me, 2)
    tile = 512
    chunks = part.shape[2] // tile

    def chunk(t):
        return pl.ds(pl.multiple_of(t * tile, tile), tile)

    def loads(t):
        return pltpu.make_async_copy(
            weight_hbm.at[:, chunk(t)], weight.at[:, chunk(t)], w_sem.at[t]
        )

    def load(t, carry):
        loads(t).start()
        return carry

    lax.fori_loop(0, chunks, load, 0)

    peers = []
    for dy, dh in ((1, 0), (3, 0), (0, 1), (2, 0), (1, 1), (3, 1), (2, 1)):
        to = lax.rem(me_y + dy, 4) * 2 + lax.rem(me_h + dh, 2)
        source = lax.rem(me_y + 4 - dy, 4) * 2 + lax.rem(me_h + dh, 2)
        peers.append((to, source))

    barrier = pltpu.get_barrier_semaphore()
    for to, _ in peers:
        pl.semaphore_signal(barrier, inc=1, device_id={"head": to}, device_id_type=MESH_ID)

    def sends(i, t):
        to = peers[i][0]
        return pltpu.make_async_remote_copy(
            src_ref=part.at[to, :, chunk(t)],
            dst_ref=got.at[i, :, chunk(t)],
            send_sem=send_sem.at[t, i],
            recv_sem=recv_sem.at[t, i],
            device_id={"head": to},
            device_id_type=MESH_ID,
        )

    attended = att_ref[...].reshape(8 * 32, att_ref.shape[3])
    pl.semaphore_wait(barrier, 7)

    def one_chunk(t, carry):
        loads(t).wait()
        value = jnp.dot(attended, weight[:, chunk(t)], preferred_element_type=jnp.float32)
        part[:, :, chunk(t)] = value.astype(jnp.bfloat16).reshape(8, 32, tile)
        for i in range(7):
            sends(i, t).start()
        return carry

    lax.fori_loop(0, chunks, one_chunk, 0)

    def add_chunk(t, square):
        for i in range(7):
            sends(i, t).wait_recv()
        value = part[me, :, chunk(t)].astype(jnp.float32)
        for i in range(7):
            value = value + got[i, :, chunk(t)].astype(jnp.float32)
        total[:, chunk(t)] = value
        return square + jnp.sum(value * value, axis=1, keepdims=True)

    square = lax.fori_loop(0, chunks, add_chunk, jnp.zeros((32, 1), jnp.float32))
    inv_rms = lax.rsqrt(square / part.shape[2] + norm_eps)

    def mix_tile(n, carry):
        columns = pl.ds(pl.multiple_of(n * tile, tile), tile)
        value = gain_ref[:, columns] * total[:, columns] * inv_rms
        for r in range(2):
            rows = value[r * 16 : (r + 1) * 16]
            out_ref[r, :, columns] = (residual_ref[r, :, columns].astype(jnp.float32) + rows).astype(
                jnp.bfloat16
            )
        return carry

    lax.fori_loop(0, chunks, mix_tile, 0)

    def drain(t, carry):
        for i in range(7):
            sends(i, t).wait_send()
        return carry

    lax.fori_loop(0, chunks, drain, 0)


def project_and_mix(attended, weight_rows, residual, post_gain):
    depth, width = weight_rows.shape
    vmem = pl.BlockSpec(memory_space=pltpu.VMEM)
    return pl.pallas_call(
        project_kernel,
        name="project_and_mix",
        out_shape=jax.ShapeDtypeStruct(residual.shape, jnp.bfloat16),
        in_specs=[vmem, pl.BlockSpec(memory_space=pl.ANY), vmem, vmem],
        out_specs=vmem,
        scratch_shapes=[
            pltpu.VMEM((depth, width), jnp.bfloat16),
            pltpu.VMEM((8, 32, width), jnp.bfloat16),
            pltpu.VMEM((7, 32, width), jnp.bfloat16),
            pltpu.VMEM((32, width), jnp.float32),
            pltpu.SemaphoreType.DMA((width // 512,)),
            pltpu.SemaphoreType.DMA((width // 512, 7)),
            pltpu.SemaphoreType.DMA((width // 512, 7)),
        ],
        compiler_params=pltpu.CompilerParams(collective_id=1, has_side_effects=True),
    )(attended, weight_rows, residual, post_gain.reshape(1, width))


def shards(
    queries,
    new_keys,
    new_values,
    pool_keys,
    pool_values,
    page_table,
    cache_len,
    out_weight,
    residual,
    post_gain,
):
    heads, dim, width = out_weight.shape
    attended = gather_and_attend(
        queries, new_keys, new_values, pool_keys, pool_values, page_table, cache_len
    )
    return project_and_mix(attended, out_weight.reshape(heads * dim, width), residual, post_gain)


def solution(mesh):
    placed = (
        P(None, "blk", "head", None),
        P(None, "blk", "head", None),
        P(None, "blk", "head", None),
        P("blk", None, "head", None),
        P("blk", None, "head", None),
        P(),
        P(),
        P("head", None, None),
        P(None, ("blk", "head"), None),
        P(),
    )
    return jax.shard_map(
        shards,
        mesh=mesh,
        in_specs=placed,
        out_specs=P(None, ("blk", "head"), None),
        check_vma=False,
    )
```

```python
import functools

import jax
import jax.numpy as jnp
from jax import lax
from jax.experimental import pallas as pl
from jax.experimental.pallas import tpu as pltpu
from jax.sharding import PartitionSpec as P

soft_cap = 50.0
score_scale = 144.0 ** (-0.5)
norm_eps = 1e-06
log2_e = 1.4426950408889634

MESH_ID = pl.DeviceIdType.MESH


def attend_kernel(
    zs_n,
    tok,
    kv_hbm,
    q_hbm,
    table_ref,
    length_ref,
    out_ref,
    kvbuf,
    qall,
    acc,
    seen,
    first,
    att_send,
    att_recv,
    local_sem,
    send_sem,
    recv_sem,
    x_send,
    x_recv,
):
    blk = lax.axis_index("blk")
    me_c = lax.rem(blk, 2)
    me_z = lax.rem(blk // 2, zs_n)
    me_x = blk // (2 * zs_n)

    def place(x, z, c):
        return {"blk": (x * zs_n + z) * 2 + c}

    right = place(me_x, lax.rem(me_z + 1, zs_n), me_c)
    left = place(me_x, lax.rem(me_z + zs_n - 1, zs_n), me_c)
    sibling = place(me_x, me_z, 1 - me_c)
    partner = place(1 - me_x, me_z, me_c)

    barrier = pltpu.get_barrier_semaphore()
    for other in (right, left, sibling, partner):
        pl.semaphore_signal(barrier, inc=1, device_id=other, device_id_type=MESH_ID)

    own_kv = pltpu.make_async_copy(kv_hbm.at[me_x], kvbuf.at[me_c, me_x, me_z], local_sem.at[0])
    own_q = pltpu.make_async_copy(q_hbm.at[me_x], qall.at[me_x], local_sem.at[1])
    own_kv.start()
    own_q.start()
    pl.semaphore_wait(barrier, 4)

    q_swap = pltpu.make_async_remote_copy(
        src_ref=q_hbm.at[1 - me_x],
        dst_ref=qall.at[me_x],
        send_sem=x_send.at[0],
        recv_sem=x_recv.at[0],
        device_id=partner,
        device_id_type=MESH_ID,
    )

    def kv_swap(h):
        return pltpu.make_async_remote_copy(
            src_ref=kv_hbm.at[1 - me_x, h],
            dst_ref=kvbuf.at[me_c, me_x, me_z, h],
            send_sem=x_send.at[2 + h],
            recv_sem=x_recv.at[2 + h],
            device_id=partner,
            device_id_type=MESH_ID,
        )

    def kv_swap_landed(h):
        here = kvbuf.at[me_c, 1 - me_x, me_z, h]
        pltpu.make_async_remote_copy(
            src_ref=here,
            dst_ref=here,
            send_sem=x_send.at[2 + h],
            recv_sem=x_recv.at[2 + h],
            device_id=partner,
            device_id_type=MESH_ID,
        ).wait_recv()

    kv_swap(0).start()
    kv_swap(1).start()
    q_swap.start()

    def forward(way, device, x, z):
        return pltpu.make_async_remote_copy(
            src_ref=kvbuf.at[me_c, x, z],
            dst_ref=kvbuf.at[me_c, x, z],
            send_sem=send_sem.at[way, x, z],
            recv_sem=recv_sem.at[me_c, x, z],
            device_id=device,
            device_id_type=MESH_ID,
        )

    def forward_half(way, device, x, z, h):
        return pltpu.make_async_remote_copy(
            src_ref=kvbuf.at[me_c, x, z, h],
            dst_ref=kvbuf.at[me_c, x, z, h],
            send_sem=send_sem.at[way, x, z],
            recv_sem=recv_sem.at[me_c, x, z],
            device_id=device,
            device_id_type=MESH_ID,
        )

    def first_sends():
        for way, device in ((0, right), (1, left), (2, sibling)):
            pltpu.make_async_remote_copy(
                src_ref=kv_hbm.at[me_x],
                dst_ref=kvbuf.at[me_c, me_x, me_z],
                send_sem=send_sem.at[way, me_x, me_z],
                recv_sem=recv_sem.at[me_c, me_x, me_z],
                device_id=device,
                device_id_type=MESH_ID,
            ).start()

    first_sends()

    def landed(c, x, z):
        pltpu.make_async_remote_copy(
            src_ref=kvbuf.at[c, x, z],
            dst_ref=kvbuf.at[c, x, z],
            send_sem=x_send.at[1],
            recv_sem=recv_sem.at[c, x, z],
            device_id=sibling,
            device_id_type=MESH_ID,
        ).wait_recv()

    last = zs_n

    def steps_right(k):
        x = jnp.where(lax.rem(k, 2) == 1, 1 - me_x, me_x)
        return x, lax.rem(me_z - k // 2 + zs_n, zs_n)

    def steps_left(k):
        x = jnp.where((lax.rem(k, 2) == 1) | (k == last), 1 - me_x, me_x)
        return x, lax.rem(me_z + k // 2, zs_n)

    def goes_right(k):
        return k <= last - 2

    def goes_left(k):
        return (k != last - 2) & (k != last)


    pages, slots = first.shape[0], table_ref.shape[1]
    page_id = lax.broadcasted_iota(jnp.int32, (pages, slots), 0)
    slot_id = lax.broadcasted_iota(jnp.int32, (pages, slots), 1).astype(jnp.float32)
    offset = lax.broadcasted_iota(jnp.int32, (pages, tok), 1)
    for r in range(2):
        match = page_id == table_ref[r : r + 1, :]
        slot = jnp.sum(jnp.where(match, slot_id, 0.0), axis=1, keepdims=True).astype(jnp.int32)
        owned = jnp.sum(jnp.where(match, 1.0, 0.0), axis=1, keepdims=True)
        visible = slot * tok + offset < length_ref[r]
        seen[r] = jnp.where(visible, owned, 0.0)
        if r == 0:
            first[...] = jnp.broadcast_to(owned, (pages, tok))
    acc[...] = jnp.zeros_like(acc)

    rows = 2 * tok
    lane = lax.broadcasted_iota(jnp.int32, (rows, tok), 1)
    row = lax.broadcasted_iota(jnp.int32, (rows, tok), 0)
    ahead = lax.rem(row, tok) - lane

    def weigh(scores):
        capped = jnp.tanh(scores * (score_scale / soft_cap))
        return jnp.exp2(capped * (soft_cap * log2_e))

    ones = jnp.ones((3 * tok, 128), jnp.bfloat16)

    def dots(a, b):
        return lax.dot_general(
            a, b, (((1,), (1,)), ((), ())), preferred_element_type=jnp.float32
        )

    def attend(c, x, z, which):
        key_block = (x * zs_n + z) * 2 + c
        for qx in which:
            query_block = (qx * zs_n + me_z) * 2 + me_c
            w_page = []
            for p in range(2):
                pick = first[pl.ds(2 * key_block + p, 1), :].astype(jnp.bfloat16)
                query = qall[qx, 0] * pick + qall[qx, 1] * (1 - pick)
                w_page.append(weigh(dots(query, kvbuf[c, x, z, 0, pl.ds((1 + p) * tok, tok), :])))
            for r in range(2):
                w_new = jnp.where(
                    ahead >= (key_block - query_block) * tok,
                    weigh(dots(qall[qx, r], kvbuf[c, x, z, 0, pl.ds(r * 3 * tok, tok), :])),
                    0.0,
                )
                w_pool = [w_page[p] * seen[r, pl.ds(2 * key_block + p, 1), :] for p in range(2)]
                both = [w_new] + w_pool if r == 0 else w_pool + [w_new]
                weights = jnp.concatenate(both, axis=1).astype(jnp.bfloat16)
                values = jnp.concatenate(
                    [kvbuf[c, x, z, 1, pl.ds(r * tok, 3 * tok), :], ones], axis=1
                )
                acc[qx, r] += jnp.dot(weights, values, preferred_element_type=jnp.float32)

    own_kv.wait()
    for h in range(2):
        kv_swap_landed(h)
        forward_half(0, right, 1 - me_x, me_z, h).start()
        forward_half(1, left, 1 - me_x, me_z, h).start()
    forward(2, sibling, 1 - me_x, me_z).start()
    own_q.wait()
    q_swap.wait_recv()

    def receive(k):
        rx, rz = steps_right(k)
        lx, lz = steps_left(k)
        landed(me_c, rx, rz)

        @pl.when(goes_right(k))
        def _():
            forward(0, right, rx, rz).start()

        landed(me_c, lx, lz)

        @pl.when(goes_left(k))
        def _():
            forward(1, left, lx, lz).start()

        forward(2, sibling, rx, rz).start()
        forward(2, sibling, lx, lz).start()

    def one_step(k, carry):
        rx, rz = steps_right(k)
        lx, lz = steps_left(k)
        own = k <= 1

        @pl.when(k > 1)
        def _():
            receive(k)

        def one_shard(i, carry):
            mine = jnp.where(own, 1, 2) > i
            c = jnp.where(mine, me_c, 1 - me_c)
            from_left = own | (lax.rem(i, 2) == 0)
            x = jnp.where(from_left, rx, lx)
            z = jnp.where(from_left, rz, lz)

            @pl.when(jnp.logical_not(mine))
            def _():
                landed(c, x, z)

            attend(c, x, z, (0, 1))
            return carry

        lax.fori_loop(0, jnp.where(own, 2, 4), one_shard, 0)
        return carry

    lax.fori_loop(0, last, one_step, 0)

    def finished(qx, r):
        total = acc[qx, r]
        return (total[:, :128] / total[:, 128:]).astype(jnp.bfloat16)

    att_swap = pltpu.make_async_remote_copy(
        src_ref=att_send,
        dst_ref=att_recv,
        send_sem=x_send.at[1],
        recv_sem=x_recv.at[1],
        device_id=partner,
        device_id_type=MESH_ID,
    )

    receive(last)
    end_rx, end_rz = steps_right(last)
    end_lx, end_lz = steps_left(last)

    def end_shard(i, carry):
        mine = lax.rem(i, 4) < 2
        c = jnp.where(mine, me_c, 1 - me_c)
        from_left = lax.rem(i, 2) == 0
        x = jnp.where(from_left, end_rx, end_lx)
        z = jnp.where(from_left, end_rz, end_lz)

        @pl.when((i == 2) | (i == 3))
        def _():
            landed(c, x, z)

        attend(c, x, z, (jnp.where(i < 4, 1 - me_x, me_x),))

        @pl.when(i == 3)
        def _():
            for r in range(2):
                att_send[r] = finished(1 - me_x, r)
            att_swap.start()

        return carry

    lax.fori_loop(0, 8, end_shard, 0)

    share = tok // 8

    def put(x, r, value):
        for g in range(2):
            columns = pl.ds(pl.multiple_of((2 * x + g) * 128, 128), 128)
            out_ref[:, r, :, columns] = value[g * tok : (g + 1) * tok].reshape(8, share, 128)

    for r in range(2):
        put(me_x, r, finished(me_x, r))
    att_swap.wait()
    for r in range(2):
        put(1 - me_x, r, att_recv[r])

    q_swap.wait_send()
    kv_swap(0).wait_send()
    kv_swap(1).wait_send()

    def drain(k, carry):
        rx, rz = steps_right(k)
        lx, lz = steps_left(k)

        @pl.when(goes_right(k))
        def _():
            forward(0, right, rx, rz).wait_send()

        @pl.when(goes_left(k))
        def _():
            forward(1, left, lx, lz).wait_send()

        forward(2, sibling, rx, rz).wait_send()

        @pl.when(k > 1)
        def _():
            forward(2, sibling, lx, lz).wait_send()

        return carry

    lax.fori_loop(0, last + 1, drain, 0)


def lay_out_kernel(q_ref, nk_ref, nv_ref, pk_ref, pv_ref, kv_ref, q_out):
    def by_head(ref, i, heads):
        rows = ref.shape[1]
        tok = rows // heads
        row = lax.broadcasted_iota(jnp.int32, (rows, rows), 0)
        column = lax.broadcasted_iota(jnp.int32, (rows, rows), 1)
        source = lax.rem(row, tok) * heads + row // tok
        order = jnp.where(source == column, 1.0, 0.0).astype(jnp.bfloat16)
        moved = jnp.dot(order, ref[i], preferred_element_type=jnp.float32)
        return moved.astype(jnp.bfloat16)

    tok = nk_ref.shape[1] // 2
    for n, (new, pool) in enumerate(((nk_ref, pk_ref), (nv_ref, pv_ref))):
        for ref, i, at in ((new, 0, 0), (pool, 0, 1), (pool, 1, 2), (new, 1, 3)):
            moved = by_head(ref, i, 2)
            for k in range(2):
                kv_ref[k, n, at * tok : (at + 1) * tok] = moved[k * tok : (k + 1) * tok]
    for r in range(2):
        moved = by_head(q_ref, r, 4)
        for k in range(2):
            q_out[k, r] = moved[2 * k * tok : 2 * (k + 1) * tok]


def lay_out(queries, new_keys, new_values, pool_keys, pool_values):
    req, tok, heads, dim = queries.shape
    rows = [a.reshape(2, -1, dim) for a in (queries, new_keys, new_values, pool_keys, pool_values)]
    vmem = pl.BlockSpec(memory_space=pltpu.VMEM)
    return pl.pallas_call(
        lay_out_kernel,
        name="lay_out",
        out_shape=(
            jax.ShapeDtypeStruct((2, 2, 4 * tok, dim), jnp.bfloat16),
            jax.ShapeDtypeStruct((2, req, 2 * tok, dim), jnp.bfloat16),
        ),
        in_specs=[vmem] * 5,
        out_specs=(vmem, vmem),
    )(*rows)


def gather_and_attend(queries, new_keys, new_values, pool_keys, pool_values, page_table, cache_len):
    req, tok, heads, dim = queries.shape
    zs_n = lax.axis_size("blk") // 4
    kv, q = lay_out(queries, new_keys, new_values, pool_keys, pool_values)
    pages = 2 * lax.axis_size("blk")

    hbm = pl.BlockSpec(memory_space=pl.ANY)
    vmem = pl.BlockSpec(memory_space=pltpu.VMEM)
    return pl.pallas_call(
        functools.partial(attend_kernel, zs_n, tok),
        name="gather_and_attend",
        out_shape=jax.ShapeDtypeStruct((8, req, tok // 8, heads * dim), jnp.bfloat16),
        in_specs=[hbm, hbm, vmem, pl.BlockSpec(memory_space=pltpu.SMEM)],
        out_specs=vmem,
        scratch_shapes=[
            pltpu.VMEM((2, 2, zs_n, 2, 4 * tok, dim), jnp.bfloat16),
            pltpu.VMEM((2, req, 2 * tok, dim), jnp.bfloat16),
            pltpu.VMEM((2, req, 2 * tok, 2 * dim), jnp.float32),
            pltpu.VMEM((req, pages, tok), jnp.float32),
            pltpu.VMEM((pages, tok), jnp.float32),
            pltpu.VMEM((req, 2 * tok, dim), jnp.bfloat16),
            pltpu.VMEM((req, 2 * tok, dim), jnp.bfloat16),
            pltpu.SemaphoreType.DMA((2,)),
            pltpu.SemaphoreType.DMA((3, 2, zs_n)),
            pltpu.SemaphoreType.DMA((2, 2, zs_n)),
            pltpu.SemaphoreType.DMA((4,)),
            pltpu.SemaphoreType.DMA((4,)),
        ],
        compiler_params=pltpu.CompilerParams(collective_id=0, has_side_effects=True),
    )(kv, q, page_table, cache_len)


def project_kernel(
    att_ref, weight_hbm, residual_ref, gain_ref, out_ref, weight, part, got, total, w_sem, send_sem, recv_sem
):
    me = lax.axis_index("head")
    me_y, me_h = me // 2, lax.rem(me, 2)
    tile = 512
    chunks = part.shape[2] // tile

    def chunk(t):
        return pl.ds(pl.multiple_of(t * tile, tile), tile)

    def loads(t):
        return pltpu.make_async_copy(
            weight_hbm.at[:, chunk(t)], weight.at[:, chunk(t)], w_sem.at[t]
        )

    def load(t, carry):
        loads(t).start()
        return carry

    lax.fori_loop(0, chunks, load, 0)

    peers = []
    for dy, dh in ((1, 0), (3, 0), (0, 1), (2, 0), (1, 1), (3, 1), (2, 1)):
        to = lax.rem(me_y + dy, 4) * 2 + lax.rem(me_h + dh, 2)
        source = lax.rem(me_y + 4 - dy, 4) * 2 + lax.rem(me_h + dh, 2)
        peers.append((to, source))

    barrier = pltpu.get_barrier_semaphore()
    for to, _ in peers:
        pl.semaphore_signal(barrier, inc=1, device_id={"head": to}, device_id_type=MESH_ID)

    def sends(i, t):
        to = peers[i][0]
        return pltpu.make_async_remote_copy(
            src_ref=part.at[to, :, chunk(t)],
            dst_ref=got.at[i, :, chunk(t)],
            send_sem=send_sem.at[t, i],
            recv_sem=recv_sem.at[t, i],
            device_id={"head": to},
            device_id_type=MESH_ID,
        )

    attended = att_ref[...].reshape(8 * 32, att_ref.shape[3])
    pl.semaphore_wait(barrier, 7)

    def one_chunk(t, carry):
        loads(t).wait()
        value = jnp.dot(attended, weight[:, chunk(t)], preferred_element_type=jnp.float32)
        part[:, :, chunk(t)] = value.astype(jnp.bfloat16).reshape(8, 32, tile)
        for i in range(7):
            sends(i, t).start()
        return carry

    lax.fori_loop(0, chunks, one_chunk, 0)

    def add_chunk(t, square):
        for i in range(7):
            sends(i, t).wait_recv()
        value = part[me, :, chunk(t)].astype(jnp.float32)
        for i in range(7):
            value = value + got[i, :, chunk(t)].astype(jnp.float32)
        total[:, chunk(t)] = value
        return square + jnp.sum(value * value, axis=1, keepdims=True)

    square = lax.fori_loop(0, chunks, add_chunk, jnp.zeros((32, 1), jnp.float32))
    inv_rms = lax.rsqrt(square / part.shape[2] + norm_eps)

    def mix_tile(n, carry):
        columns = pl.ds(pl.multiple_of(n * tile, tile), tile)
        gain = [gain_ref[pl.ds(n * (tile // 128) + j, 1), :] for j in range(tile // 128)]
        value = jnp.concatenate(gain, axis=1) * total[:, columns] * inv_rms
        for r in range(2):
            rows = value[r * 16 : (r + 1) * 16]
            out_ref[r, :, columns] = (residual_ref[r, :, columns].astype(jnp.float32) + rows).astype(
                jnp.bfloat16
            )
        return carry

    lax.fori_loop(0, chunks, mix_tile, 0)

    def drain(t, carry):
        for i in range(7):
            sends(i, t).wait_send()
        return carry

    lax.fori_loop(0, chunks, drain, 0)


def project_and_mix(attended, weight_rows, residual, post_gain):
    depth, width = weight_rows.shape
    vmem = pl.BlockSpec(memory_space=pltpu.VMEM)
    return pl.pallas_call(
        project_kernel,
        name="project_and_mix",
        out_shape=jax.ShapeDtypeStruct(residual.shape, jnp.bfloat16),
        in_specs=[vmem, pl.BlockSpec(memory_space=pl.ANY), vmem, vmem],
        out_specs=vmem,
        scratch_shapes=[
            pltpu.VMEM((depth, width), jnp.bfloat16),
            pltpu.VMEM((8, 32, width), jnp.bfloat16),
            pltpu.VMEM((7, 32, width), jnp.bfloat16),
            pltpu.VMEM((32, width), jnp.float32),
            pltpu.SemaphoreType.DMA((width // 512,)),
            pltpu.SemaphoreType.DMA((width // 512, 7)),
            pltpu.SemaphoreType.DMA((width // 512, 7)),
        ],
        compiler_params=pltpu.CompilerParams(collective_id=1, has_side_effects=True),
    )(attended, weight_rows, residual, post_gain.reshape(width // 128, 128))


def shards(
    queries,
    new_keys,
    new_values,
    pool_keys,
    pool_values,
    page_table,
    cache_len,
    out_weight,
    residual,
    post_gain,
):
    heads, dim, width = out_weight.shape
    attended = gather_and_attend(
        queries, new_keys, new_values, pool_keys, pool_values, page_table, cache_len
    )
    return project_and_mix(attended, out_weight.reshape(heads * dim, width), residual, post_gain)


def solution(mesh):
    placed = (
        P(None, "blk", "head", None),
        P(None, "blk", "head", None),
        P(None, "blk", "head", None),
        P("blk", None, "head", None),
        P("blk", None, "head", None),
        P(),
        P(),
        P("head", None, None),
        P(None, ("blk", "head"), None),
        P(),
    )
    return jax.shard_map(
        shards,
        mesh=mesh,
        in_specs=placed,
        out_specs=P(None, ("blk", "head"), None),
        check_vma=False,
    )
```
